128 devices in a mesh: wide: 16 (over x, z), narrow: 8 (over y, core).
Axes of the slice: x: 4, y: 4, z: 4, core: 2. Of those that a mesh axis runs over, the one named last changes fastest.
Arguments:
- aperture: float32 [256, 128, 128], P(('wide', 'narrow')), may hold values from 0.8 to 2.5
- pressure: float32 [256, 128, 128], P(('wide', 'narrow')), may hold values from -6 to 6
- adj_source: float32 [256, 128, 128], P(('wide', 'narrow')), may hold values from -6 to 6
- trace_weight: float32 [8192, 64], P(('wide', 'narrow')), may hold values from 0.2 to 2
- end_device: int32 [8192, 2], P(('wide', 'narrow')), may hold values from 0 to 127, as said below
- end_local: int32 [8192, 2], P(('wide', 'narrow')), may hold values from 0 to 1
- trace_nodes: int32 [8192, 2, 64], P(('wide', 'narrow')), may hold values from 0 to 16383
Outputs:
- aperture_grad: float32 [256, 128, 128], P(('wide', 'narrow'))
- adjoint: float32 [256, 128, 128], P(('wide', 'narrow'))
The draws below stay inside these ranges and needn't reach their ends.
Inputs may be any that keep to these rules, and one draw needn't show every extreme that they name: `end_device`: the two ends of an intersection lie on different devices. Of the ends of the intersections owned by one device, every device holds none or exactly 2. Any two devices are joined by at most 2 intersections over all owners, and some pairs by exactly 2. `trace_nodes`: several trace nodes may share a cell.
All inputs are finite; a program needn't handle non-finite values.
Results may differ from the reference program's by a relative error of at most 0.0022.
Values sent between devices are 32-bit elements; how exact they have to be, the bound alone decides.
A program may use at most 64 MiB of HBM per device.

```python
import math
import jax
import jax.numpy as jnp

G = 128
TRACE = 64
FR_DEV = 2
SWEEPS = 3
INNER = 8
SPAN = 32
CAP = 2
IX_DEV = 64
FRACTURES = 256
IX = 8192
DEVICES = 128


def draw_end_device(key, part):
    cycle_key = jax.random.fold_in(key, 11)
    slot_key = jax.random.fold_in(key, 12)
    flip_key = jax.random.fold_in(key, 13)
    cycle = jax.random.permutation(cycle_key, DEVICES).astype(jnp.int32)
    owner = (jnp.arange(IX, dtype=jnp.int32) // IX_DEV).astype(jnp.int32)
    orders = jax.vmap(lambda k: jax.random.permutation(k, IX_DEV))(jax.random.split(slot_key, DEVICES))
    slot = (orders.reshape(IX).astype(jnp.int32) // CAP).astype(jnp.int32)
    first = cycle[(owner + slot) % DEVICES]
    second = cycle[(owner + SPAN + 2 * slot) % DEVICES]
    flip = jax.random.randint(flip_key, (IX,), 0, 2).astype(jnp.int32)
    end_zero = jnp.where(flip == 1, second, first)
    end_one = jnp.where(flip == 1, first, second)
    return jnp.stack([end_zero, end_one], axis=1).astype(jnp.int32)


def plant(drawn, own_key, low, high):
    spot = [jax.random.randint(jax.random.fold_in(own_key, axis), (), 0, length) for axis, length in enumerate(drawn.shape)]
    widest = drawn.shape.index(max(drawn.shape))
    neighbour = spot[:widest] + [(spot[widest] + 1) % drawn.shape[widest]] + spot[widest + 1:]
    return drawn.at[tuple(spot)].set(low).at[tuple(neighbour)].set(high)


def steps_of(key, dims, pieces, smallest, top_value):
    level = 1.0
    for position, parts in pieces:
        draws = jax.random.uniform(jax.random.fold_in(jax.random.fold_in(key, 6), position), (parts,), jnp.float32, smallest / len(pieces), top_value / len(pieces))
        level = level * jnp.repeat(jnp.exp(draws), dims[position] // parts).reshape((-1,) + (1,) * (len(dims) - 1 - position))
    return level


def normal_values(own_key, dims, spread, reach, cuts=(), held_as=jnp.bfloat16):
    entries = spread * jax.random.normal(own_key, dims, jnp.float32)
    if cuts:
        entries = entries * steps_of(own_key, dims, cuts, -0.22, 0.18)
    return jnp.clip(entries, -reach, reach).astype(held_as)


def setup_inputs(seed: int = 0) -> dict:
    key_of = jax.random.split(jax.random.key(seed), 8)
    return {
        "aperture": jnp.clip(jnp.exp(math.log(2.5) - 1.13943427 * jax.random.uniform(key_of[0], (FRACTURES, G, G), jnp.float32) ** steps_of(key_of[0], (FRACTURES, G, G), ((0, 128),), -0.2, 0.2)), 0.8, 2.5),
        "pressure": normal_values(key_of[1], (FRACTURES, G, G), 1.0, 6.0, ((0, 128),), jnp.float32),
        "adj_source": normal_values(key_of[2], (FRACTURES, G, G), 1.0, 6.0, ((0, 128),), jnp.float32),
        "trace_weight": jnp.clip(jnp.exp(math.log(2.0) - 2.3025851 * jax.random.uniform(key_of[3], (IX, TRACE), jnp.float32) ** steps_of(key_of[3], (IX, TRACE), ((0, 128),), -0.2, 0.2)), 0.2, 2.0),
        "end_device": draw_end_device(jax.random.fold_in(key_of[7], 71), 0),
        "end_local": plant(jax.random.randint(key_of[5], (IX, 2), 0, FR_DEV), jax.random.fold_in(key_of[5], 1), 0, FR_DEV - 1).astype(jnp.int32),
        "trace_nodes": plant(jax.random.randint(key_of[6], (IX, 2, TRACE), 0, G * G), jax.random.fold_in(key_of[6], 1), 0, (G * G) - 1).astype(jnp.int32),
    }


LEAKAGE = 0.25


def neighbours(field, face_x, face_y):
    total = jnp.pad(face_x * field[:, 1:, :], ((0, 0), (0, 1), (0, 0)))
    total = total + jnp.pad(face_x * field[:, :-1, :], ((0, 0), (1, 0), (0, 0)))
    total = total + jnp.pad(face_y * field[:, :, 1:], ((0, 0), (0, 0), (0, 1)))
    total = total + jnp.pad(face_y * field[:, :, :-1], ((0, 0), (0, 0), (1, 0)))
    return total


def face_total(face_x, face_y):
    total = jnp.pad(face_x, ((0, 0), (0, 1), (0, 0))) + jnp.pad(face_x, ((0, 0), (1, 0), (0, 0)))
    return total + jnp.pad(face_y, ((0, 0), (0, 0), (0, 1))) + jnp.pad(face_y, ((0, 0), (0, 0), (1, 0)))


def gradient_of(aperture, pressure, adjoint):
    along_x = (pressure[:, 1:, :] - pressure[:, :-1, :]) * (adjoint[:, 1:, :] - adjoint[:, :-1, :])
    along_y = (pressure[:, :, 1:] - pressure[:, :, :-1]) * (adjoint[:, :, 1:] - adjoint[:, :, :-1])
    return -(aperture * aperture / 8.0) * face_total(along_x, along_y)


def reference(aperture, pressure, adj_source, trace_weight, end_device, end_local, trace_nodes):
    conduct = aperture * aperture * aperture / 12.0
    face_x = (conduct[:, :-1, :] + conduct[:, 1:, :]) * 0.5
    face_y = (conduct[:, :, :-1] + conduct[:, :, 1:]) * 0.5
    fracture = (end_device * FR_DEV + end_local).astype(jnp.int32)
    cells = (fracture[:, :, None] * (G * G) + trace_nodes).astype(jnp.int32).reshape(-1)
    weight_end = jnp.broadcast_to(trace_weight[:, None, :], (IX, 2, TRACE)).reshape(-1)
    total_cells = FRACTURES * G * G
    trace_sum = jnp.zeros((total_cells,), jnp.float32).at[cells].add(weight_end).reshape(FRACTURES, G, G)
    inv_diag = 1.0 / (LEAKAGE + face_total(face_x, face_y) + trace_sum)
    adjoint = adj_source * inv_diag
    for sweep_step in range(SWEEPS):
        values = adjoint.reshape(-1)[cells].reshape(IX, 2, TRACE)
        source = (trace_weight[:, None, :] * values[:, ::-1, :]).reshape(-1)
        coupling = jnp.zeros((total_cells,), jnp.float32).at[cells].add(source).reshape(FRACTURES, G, G)
        forcing = adj_source + coupling
        for inner_step in range(INNER):
            adjoint = (forcing + neighbours(adjoint, face_x, face_y)) * inv_diag
    return gradient_of(aperture, pressure, adjoint), adjoint
```

```python
import itertools

import jax
import jax.numpy as jnp
import numpy as np
from jax import lax
from jax.experimental import pallas as pl
from jax.experimental.pallas import tpu as pltpu
from jax.sharding import PartitionSpec as P

SWEEPS = 3
INNER = 8
LEAKAGE = 0.25
F32 = jnp.float32
BF16 = jnp.bfloat16
MESH = pl.DeviceIdType.MESH
DEV = 128
ROWS = 8
CHUNKS = DEV // ROWS


def negated(offset):
    return tuple(-d % 4 for d in offset[:3]) + (offset[3],)


def hops(offset):
    return sum(min(d, 4 - d) for d in offset[:3])


def far_first():
    order = []
    for offset in sorted(itertools.product(range(4), range(4), range(4), range(2)), key=lambda o: (-hops(o), o)):
        if offset not in order and negated(offset) != offset:
            order += [offset, negated(offset)]
    for offset in itertools.product((0, 2), (0, 2), (0, 2), (0, 1)):
        order.append(offset)
    order.sort(key=lambda o: (-hops(o), o == (0, 0, 0, 0)))
    return order


ORDER = far_first()
BACK = [ORDER.index(negated(o)) for o in ORDER]
assert all(b // ROWS == i // ROWS for i, b in enumerate(BACK))


def codes():
    return np.array([((o[0] * 4 + o[1]) * 4 + o[2]) * 2 + o[3] for o in ORDER], np.int32)


def device_at(offset, wide, narrow):
    dx, dz, dy, dc = offset
    return (
        ((wide // 4 + dx) % 4) * 4 + (wide % 4 + dz) % 4,
        ((narrow // 2 + dy) % 4) * 2 + (narrow % 2 + dc) % 2,
    )


def moved(code, me):
    x = ((code >> 5) + (me // 32)) & 3
    z = ((code >> 3) + (me // 8)) & 3
    y = ((code >> 1) + (me // 2)) & 3
    c = (code + me) & 1
    return x * 32 + z * 8 + y * 2 + c


def iota(shape, axis):
    return lax.broadcasted_iota(jnp.int32, shape, axis)


def wait_bytes(ref, sem):
    pltpu.make_async_copy(ref, ref, sem).wait()


def dot(a, b, ca=1, cb=0):
    return lax.dot_general(a, b, (((ca,), (cb,)), ((), ())), preferred_element_type=F32)


def hilo(x):
    high = x.astype(BF16)
    return high, (x - high.astype(F32)).astype(BF16)


def kernel(
    ap_h, pr_h, src_h, tw_h, ed_h, el_h, tn_h, kc_h, kr_h,
    grad_h, adj_h,
    ap, pr, src, tw, ed, el, tn, kc, kr, in_sem, out_sem,
    msg, rmsg, snd, rcv, m_send, m_recv, v_send, v_recv,
    hot, row1, col, wgt, adj, cup, cdn, clf, crt, inv, acc, grad,
):
    wide = lax.axis_index("wide")
    narrow = lax.axis_index("narrow")
    me = wide * 8 + narrow
    barrier = pltpu.get_barrier_semaphore()
    for offset in ORDER[:-1]:
        pl.semaphore_signal(barrier, inc=1, device_id=device_at(offset, wide, narrow), device_id_type=MESH)
    pairs = [(ed_h, ed), (el_h, el), (tn_h, tn), (tw_h, tw), (kc_h, kc), (kr_h, kr), (ap_h, ap), (src_h, src), (pr_h, pr)]
    loads = [pltpu.make_async_copy(a, b, in_sem.at[i]) for i, (a, b) in enumerate(pairs)]
    for load in loads:
        load.start()
    for load in loads[:6]:
        load.wait()

    at_col = moved(kc[...], me)
    at_row = moved(kr[...], me)[0:1, :].astype(F32)
    lane = iota((DEV, 128), 1)
    member = [jnp.where(at_col[:, :64] == ed[e : e + 1, :], 1.0, 0.0) for e in range(2)]
    earlier = jnp.where(iota((64, 64), 0) < iota((64, 64), 1), 1.0, 0.0).astype(BF16)
    before = dot((member[0] + member[1]).astype(BF16), earlier)
    place = [[jnp.where(before == float(s), member[e], 0.0) for e in range(2)] for s in range(2)]
    left = jnp.concatenate([place[s][e] for s in range(2) for e in range(2)], axis=1).astype(BF16)
    weight_parts = hilo(tw[...])
    right = []
    zero = jnp.zeros((64, 64), BF16)
    for s in range(2):
        for e in range(2):
            nodes = tn[:, e, :]
            parts = [((nodes >> 7) + 1).astype(F32).astype(BF16), (nodes & 127).astype(F32).astype(BF16), *weight_parts]
            right.append(
                jnp.concatenate([jnp.concatenate([x, zero] if s == 0 else [zero, x], axis=1) for x in parts], axis=1)
            )
    out = dot(left, jnp.concatenate(right, axis=0))

    def picked(s, rows):
        return sum(jnp.sum(place[s][e] * rows[e], axis=1, keepdims=True) for e in range(2))

    local_rows = [el[e : e + 1, :].astype(F32) for e in range(2)]
    other_rows = [ed[1 - e : 2 - e, :].astype(F32) + 1.0 for e in range(2)]
    local = jnp.where(lane < 64, picked(0, local_rows), picked(1, local_rows))
    cells = (out[:, 0:128] - 1.0 + 128.0 * local) * 128.0 + out[:, 128:256] + 1.0
    msg[:, 0, 0:128] = jnp.where(out[:, 0:128] > 0.5, cells, 0.0)
    msg[:, 0, 128:256] = out[:, 256:384] + out[:, 384:512]
    msg[:, 0, 256:384] = jnp.where(lane == 0, picked(0, other_rows), jnp.where(lane == 1, picked(1, other_rows), 0.0))

    pl.semaphore_wait(barrier, DEV - 1)
    for i, offset in enumerate(ORDER[:-1]):
        pltpu.make_async_remote_copy(
            src_ref=msg.at[i],
            dst_ref=rmsg.at[BACK[i]],
            send_sem=m_send,
            recv_sem=m_recv,
            device_id=device_at(offset, wide, narrow),
            device_id_type=MESH,
        ).start()
    rmsg[DEV - 1] = msg[DEV - 1]
    for s in range(SWEEPS):
        rcv[s, DEV - 1] = jnp.zeros((1, 128), F32)

    for load in loads[6:]:
        load.wait()
    grid_row = iota((256, 128), 0)
    grid_col = iota((256, 128), 1)
    has_down = (grid_row & 127) < 127
    has_right = grid_col < 127
    conduct = ap[...].reshape(256, 128)
    conduct = conduct * conduct * conduct * (1.0 / 12.0)
    down = jnp.where(has_down, (conduct + pltpu.roll(conduct, 255, 0)) * 0.5, 0.0)
    right_face = jnp.where(has_right, (conduct + pltpu.roll(conduct, 127, 1)) * 0.5, 0.0)
    up = pltpu.roll(down, 1, 0)
    left_face = pltpu.roll(right_face, 1, 1)
    faces = LEAKAGE + (down + up + right_face + left_face)

    wait_bytes(rmsg.at[pl.ds(0, DEV - 1)], m_recv)

    cell = rmsg[:, 0, 0:128].astype(jnp.int32) - 1
    partner = rmsg[:, 0, 256:384]
    parts = [((cell >> 7) + 1).astype(F32), (cell & 127).astype(F32)]
    parts += [x.astype(F32) for x in hilo(rmsg[:, 0, 128:256])]
    hit = [jnp.where(partner[:, s : s + 1] == at_row + 1.0, 1.0, 0.0) for s in range(2)]
    order = jnp.where(at_row < at_col.astype(F32), 1.0, 0.0).astype(BF16)
    first = dot(order, (hit[0] + hit[1]).astype(BF16))
    ahead = [first, first + hit[0]]
    left, right = [], []
    for k in range(2):
        for s in range(2):
            left.append(jnp.where(ahead[s] == float(k), hit[s], 0.0).astype(BF16))
            half = (lane < 64) if k == 0 else (lane >= 64)
            right.append(
                jnp.concatenate(
                    [jnp.where(half, x if k == s else pltpu.roll(x, 64, 1), 0.0).astype(BF16) for x in parts], axis=1
                )
            )
    out = dot(jnp.concatenate(left, axis=0), jnp.concatenate(right, axis=0), 0, 0)
    row1[...] = out[:, 0:128]
    col[...] = out[:, 128:256]
    wgt[...] = out[:, 256:384] + out[:, 384:512]

    row_ids = iota((256, 128), 0).astype(F32) + 1.0
    col_ids = iota((128, 128), 0).astype(F32)

    def lanes(chunk):
        return pl.ds(pl.multiple_of(chunk * (ROWS * 128), ROWS * 128), ROWS * 128)

    def spread(chunk, values):
        tiles = []
        for i in range(ROWS):
            columns = jnp.broadcast_to(col[pl.ds(chunk * ROWS + i, 1), :], (128, 128))
            tiles.append(jnp.where(columns == col_ids, jnp.broadcast_to(values[i], (128, 128)), 0.0).astype(BF16))
        return jnp.concatenate(tiles, axis=1)

    acc[...] = jnp.zeros((256, 128), F32)

    def first_pass(chunk, carry):
        tiles = []
        for i in range(ROWS):
            rows = jnp.broadcast_to(row1[pl.ds(chunk * ROWS + i, 1), :], (256, 128))
            tiles.append(jnp.where(rows == row_ids, 1.0, 0.0).astype(BF16))
        tile = jnp.concatenate(tiles, axis=1)
        hot[:, lanes(chunk)] = tile
        values = [wgt[pl.ds(chunk * ROWS + i, 1), :] for i in range(ROWS)]
        acc[...] += dot(tile, spread(chunk, values), 1, 1)
        return carry

    lax.fori_loop(0, CHUNKS, first_pass, 0)
    inverse = 1.0 / (faces + acc[...])
    inv[...] = inverse
    cdn[...] = down * inverse
    cup[...] = up * inverse
    crt[...] = right_face * inverse
    clf[...] = left_face * inverse
    source = src[...].reshape(256, 128)
    adj[...] = source * inverse

    def sweep(step, carry):
        field = adj[...].T.astype(BF16)
        for chunk in range(CHUNKS):
            picked_rows = dot(field, hot[:, chunk * ROWS * 128 : (chunk + 1) * ROWS * 128])
            for i in range(ROWS):
                r = chunk * ROWS + i
                columns = jnp.broadcast_to(col[r : r + 1, :], (128, 128))
                chosen = jnp.where(columns == col_ids, picked_rows[:, i * 128 : (i + 1) * 128], 0.0)
                snd[step, r] = jnp.sum(chosen, axis=0, keepdims=True)
            for r in range(chunk * ROWS, min((chunk + 1) * ROWS, DEV - 1)):
                pltpu.make_async_remote_copy(
                    src_ref=snd.at[step].at[r],
                    dst_ref=rcv.at[step].at[BACK[r]],
                    send_sem=v_send.at[step],
                    recv_sem=v_recv.at[step].at[chunk],
                    device_id=device_at(ORDER[r], wide, narrow),
                    device_id_type=MESH,
                ).start()
        acc[...] = src[...].reshape(256, 128)
        for chunk in range(CHUNKS):
            count = min(ROWS, DEV - 1 - chunk * ROWS)
            wait_bytes(rcv.at[step].at[pl.ds(chunk * ROWS, count)], v_recv.at[step].at[chunk])
            values = [rcv[step, chunk * ROWS + i] * wgt[chunk * ROWS + i : chunk * ROWS + i + 1, :] for i in range(ROWS)]
            acc[...] += dot(hot[:, chunk * ROWS * 128 : (chunk + 1) * ROWS * 128], spread(chunk, values), 1, 1)
        acc[...] = acc[...] * inv[...]

        def inner(i, carry):
            now = adj[...]
            adj[...] = (
                acc[...]
                + cdn[...] * pltpu.roll(now, 255, 0)
                + cup[...] * pltpu.roll(now, 1, 0)
                + crt[...] * pltpu.roll(now, 127, 1)
                + clf[...] * pltpu.roll(now, 1, 1)
            )
            return carry

        lax.fori_loop(0, INNER, inner, 0)
        return carry

    lax.fori_loop(0, SWEEPS, sweep, 0)
    now = adj[...]
    src[...] = now.reshape(2, 128, 128)
    store = pltpu.make_async_copy(src, adj_h, out_sem.at[0])
    store.start()
    pressure = pr[...].reshape(256, 128)
    aperture = ap[...].reshape(256, 128)
    along_x = jnp.where(has_down, (pressure - pltpu.roll(pressure, 255, 0)) * (now - pltpu.roll(now, 255, 0)), 0.0)
    along_y = jnp.where(has_right, (pressure - pltpu.roll(pressure, 127, 1)) * (now - pltpu.roll(now, 127, 1)), 0.0)
    total = along_x + pltpu.roll(along_x, 1, 0) + along_y + pltpu.roll(along_y, 1, 1)
    grad[...] = (-(aperture * aperture * 0.125) * total).reshape(2, 128, 128)
    store2 = pltpu.make_async_copy(grad, grad_h, out_sem.at[1])
    store2.start()
    wait_bytes(msg.at[pl.ds(0, DEV - 1)], m_send)
    for s in range(SWEEPS):
        wait_bytes(snd.at[s].at[pl.ds(0, DEV - 1)], v_send.at[s])
    store.wait()
    store2.wait()


def body(aperture, pressure, adj_source, trace_weight, end_device, end_local, trace_nodes):
    code_col = jnp.broadcast_to(jnp.asarray(codes())[:, None], (DEV, 128))
    code_row = jnp.broadcast_to(jnp.asarray(codes())[None, :], (8, DEV))
    field = (2, 128, 128)
    any_spec = pl.BlockSpec(memory_space=pl.ANY)
    flat = pltpu.VMEM((256, 128), F32)
    scratch = [
        pltpu.VMEM(field, F32),
        pltpu.VMEM(field, F32),
        pltpu.VMEM(field, F32),
        pltpu.VMEM((64, 64), F32),
        pltpu.VMEM((2, 64), jnp.int32),
        pltpu.VMEM((2, 64), jnp.int32),
        pltpu.VMEM((64, 2, 64), jnp.int32),
        pltpu.VMEM((DEV, 128), jnp.int32),
        pltpu.VMEM((8, DEV), jnp.int32),
        pltpu.SemaphoreType.DMA((9,)),
        pltpu.SemaphoreType.DMA((2,)),
        pltpu.VMEM((DEV, 1, 384), F32),
        pltpu.VMEM((DEV, 1, 384), F32),
        pltpu.VMEM((SWEEPS, DEV, 1, 128), F32),
        pltpu.VMEM((SWEEPS, DEV, 1, 128), F32),
        pltpu.SemaphoreType.DMA,
        pltpu.SemaphoreType.DMA,
        pltpu.SemaphoreType.DMA((SWEEPS,)),
        pltpu.SemaphoreType.DMA((SWEEPS, CHUNKS)),
        pltpu.VMEM((256, DEV * 128), BF16),
        pltpu.VMEM((DEV, 128), F32),
        pltpu.VMEM((DEV, 128), F32),
        pltpu.VMEM((DEV, 128), F32),
        flat, flat, flat, flat, flat, flat, flat,
        pltpu.VMEM(field, F32),
    ]
    return pl.pallas_call(
        kernel,
        out_shape=(jax.ShapeDtypeStruct(field, F32), jax.ShapeDtypeStruct(field, F32)),
        in_specs=[any_spec] * 9,
        out_specs=(any_spec, any_spec),
        scratch_shapes=scratch,
        compiler_params=pltpu.CompilerParams(collective_id=0, has_side_effects=True, vmem_limit_bytes=48 << 20),
    )(aperture, pressure, adj_source, trace_weight, end_device.T, end_local.T, trace_nodes, code_col, code_row)


def solution(mesh):
    line = P(("wide", "narrow"), None)
    cube = P(("wide", "narrow"), None, None)
    return jax.shard_map(
        body,
        mesh=mesh,
        in_specs=(cube, cube, cube, line, line, line, cube),
        out_specs=(cube, cube),
        check_vma=False,
    )
```

```python
import functools
import itertools

import jax
import jax.numpy as jnp
import numpy as np
from jax import lax
from jax.experimental import pallas as pl
from jax.experimental.pallas import tpu as pltpu
from jax.sharding import PartitionSpec as P

SWEEPS = 3
INNER = 8
LEAKAGE = 0.25
F32 = jnp.float32
BF16 = jnp.bfloat16
MESH = pl.DeviceIdType.MESH
DEV = 128
ROWS = 8
CHUNKS = DEV // ROWS


def negated(offset):
    return tuple(-d % 4 for d in offset[:3]) + (offset[3],)


def hops(offset):
    return sum(min(d, 4 - d) for d in offset[:3])


def in_groups():
    every = list(itertools.product(range(4), range(4), range(4), range(2)))
    every.sort(key=lambda o: (-hops(o), o == HERE))
    far = [o for o in every if hops(o) > 3]
    near = [o for o in every if hops(o) < 3]
    return far + near + [o for o in every if hops(o) == 3]


HERE = (0, 0, 0, 0)
ORDER = in_groups()
SELF = ORDER.index(HERE)
OTHERS = sorted((i for i in range(DEV) if i != SELF), key=lambda i: -hops(ORDER[i]))
BACK = [ORDER.index(negated(o)) for o in ORDER]
SENT = ((0, 16), (16, 44), (44, 88), (88, 128))
RECEIVED = ((0, 44), (44, 88), (88, 128))
HEARD = (1, 0, 2)
GROUP = [next(g for g, (a, b) in enumerate(RECEIVED) if a <= i < b) for i in range(DEV)]
assert all(GROUP[b] == GROUP[i] for i, b in enumerate(BACK))
GATHERED = 2
SCATTERED = 4


def codes():
    return np.array([((o[0] * 4 + o[1]) * 4 + o[2]) * 2 + o[3] for o in ORDER], np.int32)


def device_at(offset, wide, narrow):
    dx, dz, dy, dc = offset
    return (
        ((wide // 4 + dx) % 4) * 4 + (wide % 4 + dz) % 4,
        ((narrow // 2 + dy) % 4) * 2 + (narrow % 2 + dc) % 2,
    )


def moved(code, me):
    x = ((code >> 5) + (me // 32)) & 3
    z = ((code >> 3) + (me // 8)) & 3
    y = ((code >> 1) + (me // 2)) & 3
    c = (code + me) & 1
    return x * 32 + z * 8 + y * 2 + c


def iota(shape, axis):
    return lax.broadcasted_iota(jnp.int32, shape, axis)


def wait_bytes(ref, sem):
    pltpu.make_async_copy(ref, ref, sem).wait()


def dot(a, b, ca=1, cb=0):
    return lax.dot_general(a, b, (((ca,), (cb,)), ((), ())), preferred_element_type=F32)


def hilo(x):
    high = x.astype(BF16)
    return high, (x - high.astype(F32)).astype(BF16)


def kernel(
    ap_h, pr_h, src_h, tw_h, ed_h, el_h, tn_h, kr_h,
    grad_h, adj_h,
    ap, pr, src, tw, ed, el, tn, kr, in_sem, out_sem,
    msg, rmsg, snd, rcv, m_send, m_recv, v_send, v_recv,
    hot, row1, col, wgt, adj, cup, cdn, clf, crt, inv, acc, grad,
):
    wide = lax.axis_index("wide")
    narrow = lax.axis_index("narrow")
    me = wide * 8 + narrow
    barrier = pltpu.get_barrier_semaphore()
    for i in OTHERS:
        pl.semaphore_signal(barrier, inc=1, device_id=device_at(ORDER[i], wide, narrow), device_id_type=MESH)
    pairs = [(ed_h, ed), (el_h, el), (tn_h, tn), (tw_h, tw), (kr_h, kr), (ap_h, ap), (src_h, src), (pr_h, pr)]
    loads = [pltpu.make_async_copy(a, b, in_sem.at[i]) for i, (a, b) in enumerate(pairs)]
    for load in loads:
        load.start()
    for load in loads[:5]:
        load.wait()

    places = moved(kr[...], me).astype(F32)
    at_row = places[0:1, :]
    at_col = jnp.broadcast_to(at_row, (DEV, 128)).T
    lane = iota((DEV, 128), 1)
    member = [jnp.where(at_col[:, :64] == ed[e : e + 1, :].astype(F32), 1.0, 0.0) for e in range(2)]
    earlier = jnp.where(iota((64, 64), 0) < iota((64, 64), 1), 1.0, 0.0).astype(BF16)
    before = dot((member[0] + member[1]).astype(BF16), earlier)
    place = [[jnp.where(before == float(s), member[e], 0.0) for e in range(2)] for s in range(2)]
    left = jnp.concatenate([place[s][e] for s in range(2) for e in range(2)], axis=1).astype(BF16)
    weight_parts = hilo(tw[...])
    right = []
    zero = jnp.zeros((64, 64), BF16)
    for s in range(2):
        for e in range(2):
            nodes = tn[:, e, :]
            parts = [((nodes >> 7) + 1).astype(F32).astype(BF16), (nodes & 127).astype(F32).astype(BF16), *weight_parts]
            right.append(
                jnp.concatenate([jnp.concatenate([x, zero] if s == 0 else [zero, x], axis=1) for x in parts], axis=1)
            )
    out = dot(left, jnp.concatenate(right, axis=0))

    def picked(s, rows):
        return sum(jnp.sum(place[s][e] * rows[e], axis=1, keepdims=True) for e in range(2))

    local_rows = [el[e : e + 1, :].astype(F32) for e in range(2)]
    other_rows = [ed[1 - e : 2 - e, :].astype(F32) + 1.0 for e in range(2)]
    local = jnp.where(lane < 64, picked(0, local_rows), picked(1, local_rows))
    cells = (out[:, 0:128] - 1.0 + 128.0 * local) * 128.0 + out[:, 128:256] + 1.0
    msg[:, 0, 0:128] = jnp.where(out[:, 0:128] > 0.5, cells, 0.0)
    msg[:, 0, 128:256] = out[:, 256:384] + out[:, 384:512]
    msg[:, 0, 256:384] = jnp.where(lane == 0, picked(0, other_rows), jnp.where(lane == 1, picked(1, other_rows), 0.0))

    pl.semaphore_wait(barrier, DEV - 1)
    for i in OTHERS:
        pltpu.make_async_remote_copy(
            src_ref=msg.at[i],
            dst_ref=rmsg.at[BACK[i]],
            send_sem=m_send,
            recv_sem=m_recv,
            device_id=device_at(ORDER[i], wide, narrow),
            device_id_type=MESH,
        ).start()
    rmsg[SELF] = msg[SELF]
    for s in range(SWEEPS):
        rcv[s, SELF] = jnp.zeros((1, 128), F32)

    for load in loads[5:]:
        load.wait()
    grid_row = iota((256, 128), 0)
    grid_col = iota((256, 128), 1)
    has_down = (grid_row & 127) < 127
    has_right = grid_col < 127
    conduct = ap[...].reshape(256, 128)
    conduct = conduct * conduct * conduct * (1.0 / 12.0)
    down = jnp.where(has_down, (conduct + pltpu.roll(conduct, 255, 0)) * 0.5, 0.0)
    right_face = jnp.where(has_right, (conduct + pltpu.roll(conduct, 127, 1)) * 0.5, 0.0)
    up = pltpu.roll(down, 1, 0)
    left_face = pltpu.roll(right_face, 1, 1)
    faces = LEAKAGE + (down + up + right_face + left_face)

    wait_bytes(rmsg.at[pl.ds(0, DEV - 1)], m_recv)

    cell = rmsg[:, 0, 0:128].astype(jnp.int32) - 1
    partner = rmsg[:, 0, 256:384]
    parts = [((cell >> 7) + 1).astype(F32), (cell & 127).astype(F32)]
    parts += [x.astype(F32) for x in hilo(rmsg[:, 0, 128:256])]
    hit = [jnp.where(partner[:, s : s + 1] == at_row + 1.0, 1.0, 0.0) for s in range(2)]
    order = jnp.where(at_row < at_col, 1.0, 0.0).astype(BF16)
    first = dot(order, (hit[0] + hit[1]).astype(BF16))
    ahead = [first, first + hit[0]]
    left, right = [], []
    for k in range(2):
        for s in range(2):
            left.append(jnp.where(ahead[s] == float(k), hit[s], 0.0).astype(BF16))
            half = (lane < 64) if k == 0 else (lane >= 64)
            right.append(
                jnp.concatenate(
                    [jnp.where(half, x if k == s else pltpu.roll(x, 64, 1), 0.0).astype(BF16) for x in parts], axis=1
                )
            )
    out = dot(jnp.concatenate(left, axis=0), jnp.concatenate(right, axis=0), 0, 0)
    row1[...] = out[:, 0:128]
    col[...] = out[:, 128:256]
    wgt[...] = out[:, 256:384] + out[:, 384:512]

    row_ids = (iota((256, 128), 0).astype(F32) + 1.0).astype(BF16)
    one, nought = jnp.ones((), BF16), jnp.zeros((), BF16)
    col_ids = iota((128, 128), 0).astype(F32)

    def spread(start, values):
        tiles = []
        for i, value in enumerate(values):
            columns = jnp.broadcast_to(col[start + i : start + i + 1, :], (128, 128))
            tiles.append(jnp.where(columns == col_ids, jnp.broadcast_to(value, (128, 128)), 0.0).astype(BF16))
        return jnp.concatenate(tiles, axis=1)

    total = faces
    for chunk in range(CHUNKS):
        tiles = []
        for i in range(ROWS):
            rows = jnp.broadcast_to(row1[chunk * ROWS + i : chunk * ROWS + i + 1, :].astype(BF16), (256, 128))
            tiles.append(jnp.where(rows == row_ids, one, nought))
        tile = jnp.concatenate(tiles, axis=1)
        hot[:, chunk * ROWS * 128 : (chunk + 1) * ROWS * 128] = tile
        values = [wgt[chunk * ROWS + i : chunk * ROWS + i + 1, :] for i in range(ROWS)]
        total = total + dot(tile, spread(chunk * ROWS, values), 1, 1)
    inverse = 1.0 / total
    inv[...] = inverse
    cdn[...] = down * inverse
    cup[...] = up * inverse
    crt[...] = right_face * inverse
    clf[...] = left_face * inverse
    source = src[...].reshape(256, 128)
    adj[...] = source * inverse

    def sweep(step, carry):
        field = adj[...].T.astype(BF16)

        def send(begin, end):
            for start in range(begin, end, GATHERED):
                picked_rows = dot(field, hot[:, start * 128 : (start + GATHERED) * 128])
                for i in range(GATHERED):
                    r = start + i
                    columns = jnp.broadcast_to(col[r : r + 1, :], (128, 128))
                    chosen = jnp.where(columns == col_ids, picked_rows[:, i * 128 : (i + 1) * 128], 0.0)
                    snd[step, r] = jnp.sum(chosen, axis=0, keepdims=True)
            for r in range(begin, end):
                if r != SELF:
                    pltpu.make_async_remote_copy(
                        src_ref=snd.at[step].at[r],
                        dst_ref=rcv.at[step].at[BACK[r]],
                        send_sem=v_send.at[step],
                        recv_sem=v_recv.at[step].at[GROUP[r]],
                        device_id=device_at(ORDER[r], wide, narrow),
                        device_id_type=MESH,
                    ).start()

        for begin, end in SENT:
            pl.when(step < SWEEPS)(functools.partial(send, begin, end))

        total = src[...].reshape(256, 128)
        for g in HEARD:
            begin, end = RECEIVED[g]
            wait_bytes(rcv.at[step].at[pl.ds(begin, end - begin - (begin <= SELF < end))], v_recv.at[step].at[g])
            for start in range(begin, end, SCATTERED):
                rows = range(start, start + SCATTERED)
                values = [rcv[step, r] * wgt[r : r + 1, :] for r in rows]
                total = total + dot(hot[:, start * 128 : (start + SCATTERED) * 128], spread(start, values), 1, 1)
        acc[...] = total * inv[...]

        def inner(i, carry):
            now = adj[...]
            adj[...] = (
                acc[...]
                + cdn[...] * pltpu.roll(now, 255, 0)
                + cup[...] * pltpu.roll(now, 1, 0)
                + crt[...] * pltpu.roll(now, 127, 1)
                + clf[...] * pltpu.roll(now, 1, 1)
            )
            return carry

        lax.fori_loop(0, INNER, inner, 0, unroll=True)
        return carry

    lax.fori_loop(0, SWEEPS, sweep, 0)
    now = adj[...]
    src[...] = now.reshape(2, 128, 128)
    store = pltpu.make_async_copy(src, adj_h, out_sem.at[0])
    store.start()
    pressure = pr[...].reshape(256, 128)
    aperture = ap[...].reshape(256, 128)
    along_x = jnp.where(has_down, (pressure - pltpu.roll(pressure, 255, 0)) * (now - pltpu.roll(now, 255, 0)), 0.0)
    along_y = jnp.where(has_right, (pressure - pltpu.roll(pressure, 127, 1)) * (now - pltpu.roll(now, 127, 1)), 0.0)
    total = along_x + pltpu.roll(along_x, 1, 0) + along_y + pltpu.roll(along_y, 1, 1)
    grad[...] = (-(aperture * aperture * 0.125) * total).reshape(2, 128, 128)
    store2 = pltpu.make_async_copy(grad, grad_h, out_sem.at[1])
    store2.start()
    wait_bytes(msg.at[pl.ds(0, DEV - 1)], m_send)
    for s in range(SWEEPS):
        wait_bytes(snd.at[s].at[pl.ds(0, DEV - 1)], v_send.at[s])
    store.wait()
    store2.wait()


def body(aperture, pressure, adj_source, trace_weight, end_device, end_local, trace_nodes):
    code_row = jnp.asarray(np.tile(codes()[None, :], (8, 1)))
    field = (2, 128, 128)
    any_spec = pl.BlockSpec(memory_space=pltpu.HBM)
    flat = pltpu.VMEM((256, 128), F32)
    scratch = [
        pltpu.VMEM(field, F32),
        pltpu.VMEM(field, F32),
        pltpu.VMEM(field, F32),
        pltpu.VMEM((64, 64), F32),
        pltpu.VMEM((2, 64), jnp.int32),
        pltpu.VMEM((2, 64), jnp.int32),
        pltpu.VMEM((64, 2, 64), jnp.int32),
        pltpu.VMEM((8, DEV), jnp.int32),
        pltpu.SemaphoreType.DMA((8,)),
        pltpu.SemaphoreType.DMA((2,)),
        pltpu.VMEM((DEV, 1, 384), F32),
        pltpu.VMEM((DEV, 1, 384), F32),
        pltpu.VMEM((SWEEPS, DEV, 1, 128), F32),
        pltpu.VMEM((SWEEPS, DEV, 1, 128), F32),
        pltpu.SemaphoreType.DMA,
        pltpu.SemaphoreType.DMA,
        pltpu.SemaphoreType.DMA((SWEEPS,)),
        pltpu.SemaphoreType.DMA((SWEEPS, len(RECEIVED))),
        pltpu.VMEM((256, DEV * 128), BF16),
        pltpu.VMEM((DEV, 128), F32),
        pltpu.VMEM((DEV, 128), F32),
        pltpu.VMEM((DEV, 128), F32),
        flat, flat, flat, flat, flat, flat, flat,
        pltpu.VMEM(field, F32),
    ]
    return pl.pallas_call(
        kernel,
        out_shape=(jax.ShapeDtypeStruct(field, F32), jax.ShapeDtypeStruct(field, F32)),
        in_specs=[any_spec] * 8,
        out_specs=(any_spec, any_spec),
        scratch_shapes=scratch,
        compiler_params=pltpu.CompilerParams(collective_id=0, has_side_effects=True, vmem_limit_bytes=64 << 20),
    )(aperture, pressure, adj_source, trace_weight, end_device.T, end_local.T, trace_nodes, code_row)


def solution(mesh):
    line = P(("wide", "narrow"), None)
    cube = P(("wide", "narrow"), None, None)
    return jax.shard_map(
        body,
        mesh=mesh,
        in_specs=(cube, cube, cube, line, line, line, cube),
        out_specs=(cube, cube),
        check_vma=False,
    )
```

```python
import functools
import itertools

import jax
import jax.numpy as jnp
import numpy as np
from jax import lax
from jax.experimental import pallas as pl
from jax.experimental.pallas import tpu as pltpu
from jax.sharding import PartitionSpec as P

SWEEPS = 3
INNER = 8
LEAKAGE = 0.25
F32 = jnp.float32
BF16 = jnp.bfloat16
MESH = pl.DeviceIdType.MESH
DEV = 128
ROWS = 8
CHUNKS = DEV // ROWS


def negated(offset):
    return tuple(-d % 4 for d in offset[:3]) + (offset[3],)


def hops(offset):
    return sum(min(d, 4 - d) for d in offset[:3])


def in_groups():
    every = list(itertools.product(range(4), range(4), range(4), range(2)))
    every.sort(key=lambda o: (-hops(o), o == HERE))
    far = [o for o in every if hops(o) > 3]
    near = [o for o in every if hops(o) < 3]
    return far + near + [o for o in every if hops(o) == 3]


HERE = (0, 0, 0, 0)
ORDER = in_groups()
SELF = ORDER.index(HERE)
OTHERS = sorted((i for i in range(DEV) if i != SELF), key=lambda i: -hops(ORDER[i]))
BACK = [ORDER.index(negated(o)) for o in ORDER]
SENT = ((44, 88), (0, 44), (88, 128))
RECEIVED = ((0, 44), (44, 88), (88, 128))
HEARD = (1, 0, 2)
GROUP = [next(g for g, (a, b) in enumerate(RECEIVED) if a <= i < b) for i in range(DEV)]
assert all(GROUP[b] == GROUP[i] for i, b in enumerate(BACK))
GATHERED = 2
SCATTERED = 4


def codes():
    return np.array([((o[0] * 4 + o[1]) * 4 + o[2]) * 2 + o[3] for o in ORDER], np.int32)


def device_at(offset, wide, narrow):
    dx, dz, dy, dc = offset
    return (
        ((wide // 4 + dx) % 4) * 4 + (wide % 4 + dz) % 4,
        ((narrow // 2 + dy) % 4) * 2 + (narrow % 2 + dc) % 2,
    )


def moved(code, me):
    x = ((code >> 5) + (me // 32)) & 3
    z = ((code >> 3) + (me // 8)) & 3
    y = ((code >> 1) + (me // 2)) & 3
    c = (code + me) & 1
    return x * 32 + z * 8 + y * 2 + c


def iota(shape, axis):
    return lax.broadcasted_iota(jnp.int32, shape, axis)


def wait_bytes(ref, sem):
    pltpu.make_async_copy(ref, ref, sem).wait()


def dot(a, b, ca=1, cb=0):
    return lax.dot_general(a, b, (((ca,), (cb,)), ((), ())), preferred_element_type=F32)


def hilo(x):
    high = x.astype(BF16)
    return high, (x - high.astype(F32)).astype(BF16)


def kernel(
    ap_h, src_h, tw_h, ed_h, el_h, tn_h, kr_h,
    adj_h,
    ap, src, tw, ed, el, tn, kr, in_sem, out_sem,
    msg, rmsg, snd, rcv, m_send, m_recv, v_send, v_recv,
    hot, row1, col, wgt, adj, cup, cdn, clf, crt, inv, acc,
):
    wide = lax.axis_index("wide")
    narrow = lax.axis_index("narrow")
    me = wide * 8 + narrow
    barrier = pltpu.get_barrier_semaphore()
    for i in OTHERS:
        pl.semaphore_signal(barrier, inc=1, device_id=device_at(ORDER[i], wide, narrow), device_id_type=MESH)
    pairs = [(ed_h, ed), (el_h, el), (tn_h, tn), (tw_h, tw), (kr_h, kr), (ap_h, ap), (src_h, src)]
    loads = [pltpu.make_async_copy(a, b, in_sem.at[i]) for i, (a, b) in enumerate(pairs)]
    for load in loads:
        load.start()
    for load in loads[:5]:
        load.wait()

    places = moved(kr[...], me).astype(F32)
    at_row = places[0:1, :]
    at_col = jnp.broadcast_to(at_row, (DEV, 128)).T
    lane = iota((DEV, 128), 1)
    member = [jnp.where(at_col[:, :64] == ed[e : e + 1, :].astype(F32), 1.0, 0.0) for e in range(2)]
    earlier = jnp.where(iota((64, 64), 0) < iota((64, 64), 1), 1.0, 0.0).astype(BF16)
    before = dot((member[0] + member[1]).astype(BF16), earlier)
    place = [[jnp.where(before == float(s), member[e], 0.0) for e in range(2)] for s in range(2)]
    left = jnp.concatenate([place[s][e] for s in range(2) for e in range(2)], axis=1).astype(BF16)
    weight_parts = hilo(tw[...])
    right = []
    zero = jnp.zeros((64, 64), BF16)
    for s in range(2):
        for e in range(2):
            nodes = tn[:, e, :]
            parts = [((nodes >> 7) + 1).astype(F32).astype(BF16), (nodes & 127).astype(F32).astype(BF16), *weight_parts]
            right.append(
                jnp.concatenate([jnp.concatenate([x, zero] if s == 0 else [zero, x], axis=1) for x in parts], axis=1)
            )
    out = dot(left, jnp.concatenate(right, axis=0))

    def picked(s, rows):
        return sum(jnp.sum(place[s][e] * rows[e], axis=1, keepdims=True) for e in range(2))

    local_rows = [el[e : e + 1, :].astype(F32) for e in range(2)]
    other_rows = [ed[1 - e : 2 - e, :].astype(F32) + 1.0 for e in range(2)]
    local = jnp.where(lane < 64, picked(0, local_rows), picked(1, local_rows))
    cells = (out[:, 0:128] - 1.0 + 128.0 * local) * 128.0 + out[:, 128:256] + 1.0
    msg[:, 0, 0:128] = jnp.where(out[:, 0:128] > 0.5, cells, 0.0)
    msg[:, 0, 128:256] = out[:, 256:384] + out[:, 384:512]
    msg[:, 0, 256:384] = jnp.where(lane == 0, picked(0, other_rows), jnp.where(lane == 1, picked(1, other_rows), 0.0))

    pl.semaphore_wait(barrier, DEV - 1)
    for i in OTHERS:
        pltpu.make_async_remote_copy(
            src_ref=msg.at[i],
            dst_ref=rmsg.at[BACK[i]],
            send_sem=m_send,
            recv_sem=m_recv,
            device_id=device_at(ORDER[i], wide, narrow),
            device_id_type=MESH,
        ).start()
    rmsg[SELF] = msg[SELF]
    for s in range(SWEEPS):
        rcv[s, SELF] = jnp.zeros((1, 128), F32)

    for load in loads[5:]:
        load.wait()
    grid_row = iota((256, 128), 0)
    grid_col = iota((256, 128), 1)
    has_down = (grid_row & 127) < 127
    has_right = grid_col < 127
    conduct = ap[...].reshape(256, 128)
    conduct = conduct * conduct * conduct * (1.0 / 12.0)
    down = jnp.where(has_down, (conduct + pltpu.roll(conduct, 255, 0)) * 0.5, 0.0)
    right_face = jnp.where(has_right, (conduct + pltpu.roll(conduct, 127, 1)) * 0.5, 0.0)
    up = pltpu.roll(down, 1, 0)
    left_face = pltpu.roll(right_face, 1, 1)
    faces = LEAKAGE + (down + up + right_face + left_face)

    wait_bytes(rmsg.at[pl.ds(0, DEV - 1)], m_recv)

    cell = rmsg[:, 0, 0:128].astype(jnp.int32) - 1
    partner = rmsg[:, 0, 256:384]
    parts = [((cell >> 7) + 1).astype(F32), (cell & 127).astype(F32)]
    parts += [x.astype(F32) for x in hilo(rmsg[:, 0, 128:256])]
    hit = [jnp.where(partner[:, s : s + 1] == at_row + 1.0, 1.0, 0.0) for s in range(2)]
    order = jnp.where(at_row < at_col, 1.0, 0.0).astype(BF16)
    first = dot(order, (hit[0] + hit[1]).astype(BF16))
    ahead = [first, first + hit[0]]
    left, right = [], []
    for k in range(2):
        for s in range(2):
            left.append(jnp.where(ahead[s] == float(k), hit[s], 0.0).astype(BF16))
            half = (lane < 64) if k == 0 else (lane >= 64)
            right.append(
                jnp.concatenate(
                    [jnp.where(half, x if k == s else pltpu.roll(x, 64, 1), 0.0).astype(BF16) for x in parts], axis=1
                )
            )
    out = dot(jnp.concatenate(left, axis=0), jnp.concatenate(right, axis=0), 0, 0)
    row1[...] = out[:, 0:128]
    col[...] = out[:, 128:256]
    wgt[...] = out[:, 256:384] + out[:, 384:512]

    row_ids = (iota((256, 128), 0).astype(F32) + 1.0).astype(BF16)
    one, nought = jnp.ones((), BF16), jnp.zeros((), BF16)
    col_ids = iota((128, 128), 0).astype(F32)

    def spread(start, values):
        tiles = []
        for i, value in enumerate(values):
            columns = jnp.broadcast_to(col[start + i : start + i + 1, :], (128, 128))
            tiles.append(jnp.where(columns == col_ids, jnp.broadcast_to(value, (128, 128)), 0.0).astype(BF16))
        return jnp.concatenate(tiles, axis=1)

    total = faces
    for chunk in range(CHUNKS):
        tiles = []
        for i in range(ROWS):
            rows = jnp.broadcast_to(row1[chunk * ROWS + i : chunk * ROWS + i + 1, :].astype(BF16), (256, 128))
            tiles.append(jnp.where(rows == row_ids, one, nought))
        tile = jnp.concatenate(tiles, axis=1)
        hot[:, chunk * ROWS * 128 : (chunk + 1) * ROWS * 128] = tile
        values = [wgt[chunk * ROWS + i : chunk * ROWS + i + 1, :] for i in range(ROWS)]
        total = total + dot(tile, spread(chunk * ROWS, values), 1, 1)
    inverse = 1.0 / total
    inv[...] = inverse
    cdn[...] = down * inverse
    cup[...] = up * inverse
    crt[...] = right_face * inverse
    clf[...] = left_face * inverse
    source = src[...].reshape(256, 128)
    adj[...] = source * inverse

    def sweep(step, carry):
        field = adj[...].T.astype(BF16)

        def send(begin, end):
            for start in range(begin, end, GATHERED):
                picked_rows = dot(field, hot[:, start * 128 : (start + GATHERED) * 128])
                for i in range(GATHERED):
                    r = start + i
                    columns = jnp.broadcast_to(col[r : r + 1, :], (128, 128))
                    chosen = jnp.where(columns == col_ids, picked_rows[:, i * 128 : (i + 1) * 128], 0.0)
                    snd[step, r] = jnp.sum(chosen, axis=0, keepdims=True)
            for r in range(begin, end):
                if r != SELF:
                    pltpu.make_async_remote_copy(
                        src_ref=snd.at[step].at[r],
                        dst_ref=rcv.at[step].at[BACK[r]],
                        send_sem=v_send.at[step],
                        recv_sem=v_recv.at[step].at[GROUP[r]],
                        device_id=device_at(ORDER[r], wide, narrow),
                        device_id_type=MESH,
                    ).start()

        for begin, end in SENT:
            pl.when(me < DEV)(functools.partial(send, begin, end))

        total = src[...].reshape(256, 128)
        for g in HEARD:
            begin, end = RECEIVED[g]
            wait_bytes(rcv.at[step].at[pl.ds(begin, end - begin - (begin <= SELF < end))], v_recv.at[step].at[g])
            for start in range(begin, end, SCATTERED):
                rows = range(start, start + SCATTERED)
                values = [rcv[step, r] * wgt[r : r + 1, :] for r in rows]
                total = total + dot(hot[:, start * 128 : (start + SCATTERED) * 128], spread(start, values), 1, 1)
        acc[...] = total * inv[...]

        def inner(i, carry):
            now = adj[...]
            adj[...] = (
                acc[...]
                + cdn[...] * pltpu.roll(now, 255, 0)
                + cup[...] * pltpu.roll(now, 1, 0)
                + crt[...] * pltpu.roll(now, 127, 1)
                + clf[...] * pltpu.roll(now, 1, 1)
            )
            return carry

        lax.fori_loop(0, INNER, inner, 0, unroll=True)
        return carry

    lax.fori_loop(0, SWEEPS, sweep, 0)
    now = adj[...]
    src[...] = now.reshape(2, 128, 128)
    store = pltpu.make_async_copy(src, adj_h, out_sem.at[0])
    store.start()
    wait_bytes(msg.at[pl.ds(0, DEV - 1)], m_send)
    for s in range(SWEEPS):
        wait_bytes(snd.at[s].at[pl.ds(0, DEV - 1)], v_send.at[s])
    store.wait()


def finish(ap, pr, adj, grad, out):
    has_down = (iota((256, 128), 0) & 127) < 127
    has_right = iota((256, 128), 1) < 127
    now = adj[...].reshape(256, 128)
    out[...] = adj[...]
    pressure = pr[...].reshape(256, 128)
    aperture = ap[...].reshape(256, 128)
    along_x = jnp.where(has_down, (pressure - pltpu.roll(pressure, 255, 0)) * (now - pltpu.roll(now, 255, 0)), 0.0)
    along_y = jnp.where(has_right, (pressure - pltpu.roll(pressure, 127, 1)) * (now - pltpu.roll(now, 127, 1)), 0.0)
    total = along_x + pltpu.roll(along_x, 1, 0) + along_y + pltpu.roll(along_y, 1, 1)
    grad[...] = (-(aperture * aperture * 0.125) * total).reshape(2, 128, 128)


def body(aperture, pressure, adj_source, trace_weight, end_device, end_local, trace_nodes):
    code_row = jnp.asarray(np.tile(codes()[None, :], (8, 1)))
    field = (2, 128, 128)
    any_spec = pl.BlockSpec(memory_space=pltpu.HBM)
    flat = pltpu.VMEM((256, 128), F32)
    scratch = [
        pltpu.VMEM(field, F32),
        pltpu.VMEM(field, F32),
        pltpu.VMEM((64, 64), F32),
        pltpu.VMEM((2, 64), jnp.int32),
        pltpu.VMEM((2, 64), jnp.int32),
        pltpu.VMEM((64, 2, 64), jnp.int32),
        pltpu.VMEM((8, DEV), jnp.int32),
        pltpu.SemaphoreType.DMA((7,)),
        pltpu.SemaphoreType.DMA((1,)),
        pltpu.VMEM((DEV, 1, 384), F32),
        pltpu.VMEM((DEV, 1, 384), F32),
        pltpu.VMEM((SWEEPS, DEV, 1, 128), F32),
        pltpu.VMEM((SWEEPS, DEV, 1, 128), F32),
        pltpu.SemaphoreType.DMA,
        pltpu.SemaphoreType.DMA,
        pltpu.SemaphoreType.DMA((SWEEPS,)),
        pltpu.SemaphoreType.DMA((SWEEPS, len(RECEIVED))),
        pltpu.VMEM((256, DEV * 128), BF16),
        pltpu.VMEM((DEV, 128), F32),
        pltpu.VMEM((DEV, 128), F32),
        pltpu.VMEM((DEV, 128), F32),
        flat, flat, flat, flat, flat, flat, flat,
    ]
    shape = jax.ShapeDtypeStruct(field, F32)
    adjoint = pl.pallas_call(
        kernel,
        out_shape=shape,
        in_specs=[any_spec] * 7,
        out_specs=any_spec,
        scratch_shapes=scratch,
        compiler_params=pltpu.CompilerParams(collective_id=0, has_side_effects=True, vmem_limit_bytes=64 << 20),
    )(aperture, adj_source, trace_weight, end_device.T, end_local.T, trace_nodes, code_row)
    whole = pl.BlockSpec(memory_space=pltpu.VMEM)
    return pl.pallas_call(
        finish,
        out_shape=(shape, shape),
        in_specs=[whole] * 3,
        out_specs=(whole, whole),
        compiler_params=pltpu.CompilerParams(vmem_limit_bytes=64 << 20),
    )(aperture, pressure, adjoint)


def solution(mesh):
    line = P(("wide", "narrow"), None)
    cube = P(("wide", "narrow"), None, None)
    return jax.shard_map(
        body,
        mesh=mesh,
        in_specs=(cube, cube, cube, line, line, line, cube),
        out_specs=(cube, cube),
        check_vma=False,
    )
```
